32 devices in a mesh: gx: 8 (over z, y), gy: 4 (over x, core).
Axes of the slice: x: 2, y: 2, z: 4, core: 2. Of those that a mesh axis runs over, the one named last changes fastest.
Arguments:
- tokens: bfloat16 [256, 16384], P('gy', 'gx'), may hold values from -2 to 2
- lengths: int32 [64], P('gx'), may hold values from 1 to 512, 16384 in all
- key_cache: bfloat16 [64, 512, 8, 128], P('gx', None, 'gy'), may hold values from -800 to 800
- value_cache: bfloat16 [64, 512, 8, 128], P('gx', None, 'gy'), may hold values from -6 to 6
- attn_gain: float32 [16384], P('gx'), may hold values from 0.1 to 1.9
- qkv_weight: bfloat16 [16384, 8, 10, 128], P('gx', 'gy'), may hold values from -0.046875 to 0.046875
- out_weight: bfloat16 [8192, 16384], P('gy', 'gx'), may hold values from -0.25 to 0.25
- ffn_gain: float32 [16384], P('gx'), may hold values from 0.1 to 1.9
- gate_up_weight: bfloat16 [16384, 2, 26624], P('gx', None, 'gy'), may hold values from -0.046875 to 0.046875
- down_weight: bfloat16 [26624, 16384], P('gy', 'gx'), may hold values from -0.078125 to 0.078125
Outputs:
- layer_out: float32 [256, 16384], P('gy', 'gx')
The draws below stay inside these ranges and needn't reach their ends.
Inputs may be any that keep to these rules, and one draw needn't show every extreme that they name: Request r's cache holds live entries in slots 0 to lengths[r] - 1; the largest length is exactly 512.
All inputs are finite; a program needn't handle non-finite values. No bound on the sum of `lengths` on one device may be relied on, other than what follows from the above.
Results may differ from the reference program's by a relative error of at most 0.018.
The reference program's roundings to bfloat16 on the way count: a program that leaves them out, or rounds other values in their place, can miss the bound.
Values may be sent and summed in bfloat16 or wider, within the bound.
No kernel may reach another device: no remote copies, remote signals or barrier semaphores. Data moves between devices by JAX's collectives and lax.ppermute only.
A program may use at most 256 MiB of HBM per device.

```python
import math
import jax
import jax.numpy as jnp
import numpy as np
from jax import lax

D = 16384
HD = 128
KVH = 8
GROUP = 8
FF = 26624
DRAFT = 4
CTX = 512
HQ = 64
REQUESTS = 64
TOK = 256
N_GX = 8
N_GY = 4


def draw_tokens(key, part):
    key_rows, key_cols, key_base = jax.random.split(key, 3)
    row_scales = jnp.exp(jax.random.uniform(key_rows, (TOK, 1), jnp.float32, jnp.log(0.025), jnp.log(0.25)))
    jitter = jnp.exp(jax.random.uniform(key_cols, (1, D), jnp.float32, jnp.log(0.8), jnp.log(1.25)))
    place = jnp.arange(D, dtype=jnp.float32)[None, :] / (D - 1)
    rising = jnp.exp(jnp.log(0.5) + place * jnp.log(3.0))
    baseline = jnp.clip(jax.random.normal(key_base, (TOK, D), jnp.float32), -4.0, 4.0)
    return (baseline * row_scales * rising * jitter).astype(jnp.bfloat16)


def draw_key_cache(key, part):
    key_base = jax.random.fold_in(jax.random.fold_in(key, 17), 0)
    array_shape = (REQUESTS, CTX, KVH, HD)
    values = jnp.clip(jax.random.normal(key_base, array_shape, jnp.float32), -4.0, 4.0)
    return values.astype(jnp.bfloat16)


def block_scale(rng, extent, pieces, least, high):
    level = 1.0
    for position, parts in pieces:
        draws = jax.random.uniform(jax.random.fold_in(jax.random.fold_in(rng, 6), position), (parts,), jnp.float32, least / len(pieces), high / len(pieces))
        level = level * jnp.repeat(jnp.exp(draws), extent[position] // parts).reshape((-1,) + (1,) * (len(extent) - 1 - position))
    return level


def length_profile(count, total, bound, skew):
    weights = [(1 << 20) // math.isqrt(grade ** skew) + 1 for grade in range(2, count + 1)]
    spare, given = total - bound - (count - 1), [1] * (count - 1)
    while spare > 0:
        candidates = [i for i in range(count - 1) if given[i] < bound]
        pool, budget = sum([weights[i] for i in candidates]), spare
        for i in candidates:
            more = min(bound - given[i], max(1, budget * weights[i] // pool), spare)
            given[i] = given[i] + more
            spare = spare - more
    return np.array([bound] + given)


def uneven(own_key, count, total, most, skew):
    if count == 2:
        one = jax.random.randint(own_key, (), max(1, total - most), min(most, total - 1) + 1)
        return jnp.stack([one, total - one])
    sizes = jnp.asarray(length_profile(count, total, most, skew), jnp.int32)
    couples = (count - 1) // 2
    source_of, taker = sizes[1:1 + 2 * couples:2], sizes[2:2 + 2 * couples:2]
    room = jnp.minimum(source_of - 1, most - taker)
    moved = jax.random.randint(jax.random.fold_in(own_key, 1), (couples,), 0, 1 << 20) % (room + 1)
    sizes = sizes.at[1:1 + 2 * couples:2].set(source_of - moved).at[2:2 + 2 * couples:2].set(taker + moved)
    return sizes[jax.random.permutation(jax.random.fold_in(own_key, 2), count)]


def gaussian(key, dims, spread, bound, cuts=(), kind=jnp.bfloat16):
    factor_of = block_scale(key, dims, cuts, -0.22, 0.18) if cuts else 1.0
    entries = jax.random.normal(key, dims, jnp.float32) * spread * factor_of
    return jnp.minimum(jnp.maximum(entries, -bound), bound).astype(kind)


def setup_inputs(seed: int = 0) -> dict:
    key_of = jax.random.split(jax.random.key(seed), 11)
    return {
        "tokens": draw_tokens(jax.random.fold_in(key_of[10], 71), 0),
        "lengths": uneven(key_of[1], REQUESTS, REQUESTS * CTX // 2, CTX, 2).astype(jnp.int32),
        "key_cache": draw_key_cache(jax.random.fold_in(key_of[10], 71), 0),
        "value_cache": gaussian(key_of[3], (REQUESTS, CTX, KVH, HD), 1.0, 6.0, ((0, 8), (2, 4))),
        "attn_gain": jnp.clip(1.0 + 0.18 * jax.random.normal(key_of[4], (D,), jnp.float32), 0.1, 1.9),
        "qkv_weight": gaussian(key_of[5], (D, KVH, GROUP + 2, HD), D ** -0.5, 0.046875, ((0, 8), (1, 4))),
        "out_weight": gaussian(key_of[6], (HQ * HD, D), (HQ * HD // 16) ** -0.5, 0.25, ((0, 4), (1, 8))),
        "ffn_gain": jnp.clip(1.0 + 0.18 * jax.random.normal(key_of[7], (D,), jnp.float32), 0.1, 1.9),
        "gate_up_weight": gaussian(key_of[8], (D, 2, FF), D ** -0.5, 0.046875, ((0, 8), (2, 4))),
        "down_weight": gaussian(key_of[9], (FF, D), (FF // 4) ** -0.5, 0.078125, ((0, 4), (1, 8))),
    }


EPSILON = 1e-05
ROPE_BASE = 500000.0

def root_norm(token_rows, gain_vector):
    values = token_rows.astype(jnp.float32)
    scaling = lax.rsqrt(lax.optimization_barrier(jnp.mean(values * values, axis=1, keepdims=True)) + EPSILON)
    return (values * scaling * gain_vector.astype(jnp.float32)).astype(jnp.bfloat16)

def rotate(values, positions):
    half_size = values.shape[-1] // 2
    frequencies = jnp.power(ROPE_BASE, -jnp.arange(half_size, dtype=jnp.float32) * 2.0 / values.shape[-1])
    angles = positions[..., None] * frequencies
    cosine = jnp.cos(angles)
    sine_part = jnp.sin(angles)
    first_half = values[..., :half_size]
    second_half = values[..., half_size:]
    return jnp.concatenate([first_half * cosine - second_half * sine_part, second_half * cosine + first_half * sine_part], axis=-1)

def blocked(token_rows, weight, groups):
    block_width = weight.shape[0] // groups

    def accumulate(running, block_index):
        partial_value = jnp.dot(lax.dynamic_slice_in_dim(token_rows, block_index * block_width, block_width, 1), lax.dynamic_slice_in_dim(weight, block_index * block_width, block_width, 0), preferred_element_type=jnp.float32)
        return (running + lax.optimization_barrier(partial_value.astype(jnp.bfloat16)).astype(jnp.float32), None)
    running, unused = lax.scan(accumulate, jnp.zeros((token_rows.shape[0], weight.shape[1]), jnp.float32), jnp.arange(groups, dtype=jnp.int32))
    return running

def attend(queries, new_keys, new_values, key_cache, value_cache, lengths):
    scaling = queries.shape[-1] ** (-0.5)
    cache_scores = jnp.einsum('rjkgd,rpkd->rkgjp', queries.astype(jnp.float32), key_cache.astype(jnp.float32)) * scaling
    draft_scores = jnp.einsum('rjkgd,rikd->rkgji', queries.astype(jnp.float32), new_keys.astype(jnp.float32)) * scaling
    slots = jnp.arange(key_cache.shape[1], dtype=jnp.int32)
    cache_mask = (slots[None, :] < lengths[:, None])[:, None, None, None, :]
    order = jnp.arange(queries.shape[1], dtype=jnp.int32)
    draft_mask = (order[None, :] <= order[:, None])[None, None, None, :, :]
    cache_scores = jnp.where(cache_mask, cache_scores, -1e+30)
    draft_scores = jnp.where(draft_mask, draft_scores, -1e+30)
    row_max = jnp.maximum(lax.optimization_barrier(jnp.max(cache_scores, axis=-1)), lax.optimization_barrier(jnp.max(draft_scores, axis=-1)))[..., None]
    cache_weights = jnp.exp(cache_scores - row_max)
    draft_weights = jnp.exp(draft_scores - row_max)
    denominator = lax.optimization_barrier(jnp.sum(cache_weights, axis=-1, keepdims=True)) + lax.optimization_barrier(jnp.sum(draft_weights, axis=-1, keepdims=True))
    cache_probs = (cache_weights / denominator).astype(jnp.bfloat16)
    draft_probs = (draft_weights / denominator).astype(jnp.bfloat16)
    mixture = jnp.einsum('rkgjp,rpkd->rjkgd', cache_probs.astype(jnp.float32), value_cache.astype(jnp.float32))
    mixture = mixture + jnp.einsum('rkgji,rikd->rjkgd', draft_probs.astype(jnp.float32), new_values.astype(jnp.float32))
    return mixture.astype(jnp.bfloat16)

def reference(tokens, lengths, key_cache, value_cache, attn_gain, qkv_weight, out_weight, ffn_gain, gate_up_weight, down_weight):
    normed = root_norm(tokens, attn_gain)
    projected = blocked(normed, qkv_weight.reshape(D, -1), N_GX).reshape(REQUESTS, DRAFT, KVH, GROUP + 2, HD)
    positions = (lengths[:, None] + jnp.arange(DRAFT, dtype=jnp.int32)[None, :]).astype(jnp.float32)
    queries = rotate(projected[:, :, :, :GROUP], positions[:, :, None, None]).astype(jnp.bfloat16)
    new_keys = rotate(projected[:, :, :, GROUP], positions[:, :, None]).astype(jnp.bfloat16)
    new_values = projected[:, :, :, GROUP + 1].astype(jnp.bfloat16)
    attended = attend(queries, new_keys, new_values, key_cache, value_cache, lengths).reshape(TOK, HQ * HD)
    residual = (tokens.astype(jnp.float32) + blocked(attended, out_weight, N_GY)).astype(jnp.bfloat16)
    ffn_input = root_norm(residual, ffn_gain)
    gate_up = blocked(ffn_input, gate_up_weight.reshape(D, 2 * FF), N_GX)
    hidden = (jax.nn.silu(gate_up[:, :FF]) * gate_up[:, FF:]).astype(jnp.bfloat16)
    return residual.astype(jnp.float32) + blocked(hidden, down_weight, N_GY)
```

```python
import functools
import math

import jax
import jax.numpy as jnp
from jax import lax
from jax.experimental import pallas as pl
from jax.experimental.pallas import tpu as pltpu
from jax.sharding import PartitionSpec as P

EPSILON = 1e-05
ROPE_BASE = 500000.0
CHUNK_SHARES = (4, 4, 3, 2)


def halves(count):
    inner = max(d for d in range(1, math.isqrt(count) + 1) if count % d == 0)
    return count // inner, inner


def place(axis):
    outer, inner = halves(lax.axis_size(axis))
    index = lax.axis_index(axis)
    return outer, inner, index // inner, index % inner


def shift_outer(values, axis, step):
    outer, inner = halves(lax.axis_size(axis))
    pairs = [(o * inner + i, ((o + step) % outer) * inner + i) for o in range(outer) for i in range(inner)]
    return lax.ppermute(values, axis, pairs)


def shift_inner(values, axis, step):
    outer, inner = halves(lax.axis_size(axis))
    pairs = [(o * inner + i, o * inner + (i + step) % inner) for o in range(outer) for i in range(inner)]
    return lax.ppermute(values, axis, pairs)


def gather_relative(block, axis):
    outer, inner = halves(lax.axis_size(axis))
    line = jnp.stack([block] + [shift_outer(block, axis, s) for s in range(1, outer)])
    whole = jnp.stack([line] + [shift_inner(line, axis, s) for s in range(1, inner)])
    return whole.reshape((inner * outer,) + block.shape)


def relative_position(axis, blocks):
    outer, inner, o, i = place(axis)
    return ((i - blocks % inner) % inner) * outer + (o - blocks // inner) % outer


def targets(axis):
    outer, inner, o, i = place(axis)
    near = jnp.arange(inner, dtype=jnp.int32)[:, None]
    far = jnp.arange(outer, dtype=jnp.int32)[None, :]
    return (((o + far) % outer) * inner + (i + near) % inner).reshape(-1)


def norm_kernel(source_ref, block_ref, rows_ref, scale_ref, gain_ref, out_ref, *, size):
    for k in range(out_ref.shape[0] // size):
        rows = rows_ref[pl.ds(source_ref[k] * size, size), :].astype(jnp.float32)
        scale = scale_ref[pl.ds(block_ref[k] * size, size), :]
        out_ref[k * size:(k + 1) * size, :] = (rows * scale * gain_ref[...]).astype(jnp.bfloat16)


def gathered_norm(rows, gain, order, size):
    grid_rows, columns = lax.axis_size("gx"), rows.shape[1]
    groups = lax.axis_size("gy")
    values = rows.astype(jnp.float32)
    local = jnp.sum(values * values, axis=1)
    shares = lax.all_to_all(
        jnp.broadcast_to(local[None], (grid_rows * groups, rows.shape[0])), ("gx", "gy"), 0, 0, tiled=True
    )
    totals = jnp.sum(shares.reshape(grid_rows, groups * rows.shape[0]), axis=0)
    scale = lax.rsqrt(totals / (columns * grid_rows) + EPSILON)[:, None]
    every = gather_relative(rows, "gy").reshape(groups * rows.shape[0], columns)
    per_owner = rows.shape[0] // size
    source = relative_position("gy", order // per_owner) * per_owner + order % per_owner
    smem = pl.BlockSpec(memory_space=pltpu.SMEM)
    vmem = pl.BlockSpec(memory_space=pltpu.VMEM)
    return pl.pallas_call(
        functools.partial(norm_kernel, size=size),
        out_shape=jax.ShapeDtypeStruct(every.shape, jnp.bfloat16),
        in_specs=[smem, smem, vmem, vmem, vmem],
        out_specs=vmem,
        name="gathered_norm",
    )(source, order, every, scale, gain[None])


def rotate(values, positions):
    half_size = values.shape[-1] // 2
    frequencies = jnp.power(
        ROPE_BASE, -jnp.arange(half_size, dtype=jnp.float32) * 2.0 / values.shape[-1]
    )
    angles = positions[..., None] * frequencies
    cosine = jnp.cos(angles)
    sine_part = jnp.sin(angles)
    first_half = values[..., :half_size]
    second_half = values[..., half_size:]
    return jnp.concatenate(
        [
            first_half * cosine - second_half * sine_part,
            second_half * cosine + first_half * sine_part,
        ],
        axis=-1,
    )


def attend(queries, new_keys, new_values, key_cache, value_cache, lengths):
    scaling = queries.shape[-1] ** (-0.5)
    cache_scores = (
        jnp.einsum("rjkgd,rpkd->rkgjp", queries, key_cache, preferred_element_type=jnp.float32)
        * scaling
    )
    draft_scores = (
        jnp.einsum("rjkgd,rikd->rkgji", queries, new_keys, preferred_element_type=jnp.float32)
        * scaling
    )
    slots = jnp.arange(key_cache.shape[1], dtype=jnp.int32)
    cache_mask = (slots[None, :] < lengths[:, None])[:, None, None, None, :]
    order = jnp.arange(queries.shape[1], dtype=jnp.int32)
    draft_mask = (order[None, :] <= order[:, None])[None, None, None, :, :]
    cache_scores = jnp.where(cache_mask, cache_scores, -1e30)
    draft_scores = jnp.where(draft_mask, draft_scores, -1e30)
    row_max = jnp.maximum(jnp.max(cache_scores, axis=-1), jnp.max(draft_scores, axis=-1))[..., None]
    cache_weights = jnp.exp(cache_scores - row_max)
    draft_weights = jnp.exp(draft_scores - row_max)
    denominator = jnp.sum(cache_weights, axis=-1, keepdims=True) + jnp.sum(
        draft_weights, axis=-1, keepdims=True
    )
    cache_probs = (cache_weights / denominator).astype(jnp.bfloat16)
    draft_probs = (draft_weights / denominator).astype(jnp.bfloat16)
    mixture = jnp.einsum(
        "rkgjp,rpkd->rjkgd", cache_probs, value_cache, preferred_element_type=jnp.float32
    )
    mixture = mixture + jnp.einsum(
        "rkgji,rikd->rjkgd", draft_probs, new_values, preferred_element_type=jnp.float32
    )
    return mixture.astype(jnp.bfloat16)


def rows_kernel(*refs, steps, size, carried, final):
    order_ref, x_ref, w_ref = refs[:3]
    refs = refs[3:]
    if carried:
        base_ref, refs = refs[0], refs[1:]
    outs, total_ref = refs[:-1], refs[-1]
    step = pl.program_id(0)
    product = jnp.dot(x_ref[...], w_ref[...], preferred_element_type=jnp.float32)

    @pl.when(step == 0)
    def _():
        total_ref[...] = product + base_ref[...] if carried else product

    @pl.when(step > 0)
    def _():
        total_ref[...] += product

    @pl.when(step == steps - 1)
    def _():
        if not final:
            outs[0][...] = total_ref[...]
            return
        place_in = 0
        for out in outs:
            for k in range(out.shape[0] // size):
                picked = total_ref[pl.ds(order_ref[place_in] * size, size), :]
                out[k * size:(k + 1) * size, :] = picked.astype(jnp.bfloat16)
                place_in += 1


def rows_product(x, weight, start, base, order, size, parts):
    rows, depth = x.shape
    columns = weight.shape[1]
    block = math.gcd(math.gcd(depth, start), 512)
    steps = depth // block
    final = parts is not None
    carried = base is not None
    whole = lambda k: (0, 0)
    in_specs = [
        pl.BlockSpec(memory_space=pltpu.SMEM),
        pl.BlockSpec((rows, block), lambda k: (0, k)),
        pl.BlockSpec((block, columns), lambda k: (start // block + k, 0)),
    ]
    operands = [order, x, weight]
    if carried:
        in_specs.append(pl.BlockSpec((rows, columns), whole))
        operands.append(base)
    if final:
        shapes = [jax.ShapeDtypeStruct((rows // parts, columns), jnp.bfloat16)] * parts
    else:
        shapes = [jax.ShapeDtypeStruct((rows, columns), jnp.float32)]
    return pl.pallas_call(
        functools.partial(rows_kernel, steps=steps, size=size, carried=carried, final=final),
        grid=(steps,),
        in_specs=in_specs,
        out_specs=[pl.BlockSpec(s.shape, whole) for s in shapes],
        out_shape=shapes,
        scratch_shapes=[pltpu.VMEM((rows, columns), jnp.float32)],
        name="rows_product",
        cost_estimate=pl.CostEstimate(
            flops=2 * rows * depth * columns, bytes_accessed=2 * depth * columns, transcendentals=0
        ),
    )(*operands)


def pair_kernel(x_ref, w_ref, *outs, outer, size):
    weights = jnp.swapaxes(w_ref[...], 0, 1)
    for half in range(2):
        product = jnp.dot(x_ref[...], weights[half], preferred_element_type=jnp.float32)
        product = product.astype(jnp.bfloat16)
        for k in range(outer):
            outs[k][half] = product[k * size:(k + 1) * size, :]
        for n, out in enumerate(outs[outer:], 1):
            for k in range(outer):
                at = (n * outer + k) * size
                out[k, half] = product[at:at + size, :]


def pair_product(x, weight, start, width, outer, inner, size):
    rows, depth = x.shape
    block = math.gcd(math.gcd(width, start), 512)
    shapes = [jax.ShapeDtypeStruct((2, size, width), jnp.bfloat16)] * outer
    specs = [pl.BlockSpec((2, size, block), lambda j: (0, 0, j))] * outer
    shapes += [jax.ShapeDtypeStruct((outer, 2, size, width), jnp.bfloat16)] * (inner - 1)
    specs += [pl.BlockSpec((outer, 2, size, block), lambda j: (0, 0, 0, j))] * (inner - 1)
    return pl.pallas_call(
        functools.partial(pair_kernel, outer=outer, size=size),
        grid=(width // block,),
        in_specs=[
            pl.BlockSpec((rows, depth), lambda j: (0, 0)),
            pl.BlockSpec((depth, 2, block), lambda j: (0, 0, start // block + j)),
        ],
        out_specs=specs,
        out_shape=shapes,
        name="pair_product",
        cost_estimate=pl.CostEstimate(
            flops=4 * rows * depth * width, bytes_accessed=4 * depth * width, transcendentals=0
        ),
    )(x, weight)


def wide(values):
    return values.astype(jnp.float32)


def scatter_rows(parts, size):
    outer, inner = halves(lax.axis_size("gy"))
    total = wide(parts[0])
    for step in range(1, inner):
        total = total + wide(shift_inner(parts[step], "gy", step))
    if outer == 1:
        return total
    pieces = total.astype(jnp.bfloat16).reshape(outer, -1, total.shape[1])
    result = wide(pieces[0])
    for step in range(1, outer):
        result = result + wide(shift_outer(pieces[step], "gy", step))
    return result


def per_device(
    tokens,
    lengths,
    key_cache,
    value_cache,
    attn_gain,
    qkv_weight,
    out_weight,
    ffn_gain,
    gate_up_weight,
    down_weight,
):
    grid_rows, groups = lax.axis_size("gx"), lax.axis_size("gy")
    outer, inner = halves(grid_rows)
    token_count = tokens.shape[0] * groups
    local_rows = token_count // grid_rows
    blocks = jnp.arange(grid_rows, dtype=jnp.int32)

    head_count = qkv_weight.shape[1]
    group_size = qkv_weight.shape[2] - 2
    head_size = qkv_weight.shape[3]
    normed = gathered_norm(tokens, attn_gain, blocks, local_rows)
    partial = jnp.einsum("tk,khgd->thgd", normed, qkv_weight, preferred_element_type=jnp.float32)
    partial = partial.astype(jnp.bfloat16).reshape(grid_rows, local_rows, head_count, group_size + 2, head_size)
    shares = lax.all_to_all(partial, "gx", 0, 0, tiled=True)
    projected = jnp.sum(wide(shares), axis=0)
    request_count = lengths.shape[0]
    draft_len = local_rows // request_count
    projected = projected.reshape(request_count, draft_len, head_count, group_size + 2, head_size)
    positions = (lengths[:, None] + jnp.arange(draft_len, dtype=jnp.int32)[None, :]).astype(
        jnp.float32
    )
    queries = rotate(projected[:, :, :, :group_size], positions[:, :, None, None]).astype(
        jnp.bfloat16
    )
    new_keys = rotate(projected[:, :, :, group_size], positions[:, :, None]).astype(jnp.bfloat16)
    new_values = projected[:, :, :, group_size + 1].astype(jnp.bfloat16)
    attended = attend(queries, new_keys, new_values, key_cache, value_cache, lengths).reshape(
        local_rows, -1
    )

    every_token = gather_relative(attended, "gx").reshape(token_count, -1)
    per_owner = tokens.shape[0] // local_rows
    owned = targets("gy")[:, None] * per_owner + jnp.arange(per_owner, dtype=jnp.int32)
    back = relative_position("gx", owned.reshape(-1))
    parts = halves(groups)[1]
    pieces = rows_product(every_token, out_weight, 0, None, back, local_rows, parts)
    residual = (wide(tokens) + scatter_rows(pieces, local_rows)).astype(jnp.bfloat16)

    ffn_input = gathered_norm(residual, ffn_gain, targets("gx"), local_rows)
    unit_count = gate_up_weight.shape[2]
    grain = math.gcd(unit_count, 512)
    bounds = [0]
    for n in range(len(CHUNK_SHARES)):
        share = sum(CHUNK_SHARES[:n + 1]) * (unit_count // grain) // sum(CHUNK_SHARES)
        bounds.append(share * grain)
    total = None
    for start, stop in zip(bounds[:-1], bounds[1:]):
        made = pair_product(ffn_input, gate_up_weight, start, stop - start, outer, inner, local_rows)
        near = [wide(v) for v in made[:outer]]
        for step in range(1, inner):
            came = shift_inner(made[outer + step - 1], "gx", step)
            near = [v + wide(came[k]) for k, v in enumerate(near)]
        near = [v.astype(jnp.bfloat16) for v in near]
        summed = wide(near[0])
        for step in range(1, outer):
            summed = summed + wide(shift_outer(near[step], "gx", step))
        activated = (jax.nn.silu(summed[0]) * summed[1]).astype(jnp.bfloat16)
        hidden = gather_relative(activated, "gx").reshape(token_count, -1)
        last = stop == unit_count
        total = rows_product(
            hidden, down_weight, start, total, back, local_rows, parts if last else None
        )
        if not last:
            total = total[0]
    return wide(residual) + scatter_rows(total, local_rows)


def solution(mesh):
    placed = (
        P("gy", "gx"),
        P("gx"),
        P("gx", None, "gy", None),
        P("gx", None, "gy", None),
        P("gx"),
        P("gx", "gy", None, None),
        P("gy", "gx"),
        P("gx"),
        P("gx", None, "gy"),
        P("gy", "gx"),
    )
    return jax.shard_map(
        per_device, mesh=mesh, in_specs=placed, out_specs=P("gy", "gx"), check_vma=False
    )
```
